256 devices in a mesh: line: 32 (over z, x_hi, core), bus: 8 (over x_lo, y).
Axes of the slice: x: 4 (x_hi: 2, x_lo: 2; x = x_hi * 2 + x_lo), y: 4, z: 8, core: 2. Of those that a mesh axis runs over, the one named last changes fastest.
Arguments:
- injections: float32 [2048, 8192], P('line', 'bus'), may hold values from -6 to 6
- shift_factors: float32 [16384, 8192], P('line', 'bus'), may hold values from -0.0625 to 0.0625
- line_rating: int32 [2048, 16384], P(None, 'line'), may hold values from 40 to 159
- retention: float32 [2048, 1024], P('line', 'bus'), may hold values from 0.5 to 1
- discharge: float32 [1024], P('bus'), may hold values from 0.05 to 0.5
- profile: float32 [2048, 1024], P('line', 'bus'), may hold values from -6 to 6
- storage_bus: int32 [1024], P('bus'), may hold values from 0 to 8191, as said below
- online_hour: int32 [1024], P('bus'), may hold values from 0 to 1023
Outputs:
- bus_adjoint: float32 [2048, 8192], P('line', 'bus')
- size_grad: float32 [1024], P('bus')
The draws below stay inside these ranges and needn't reach their ends.
Inputs may be any that keep to these rules, and one draw needn't show every extreme that they name: `storage_bus`: unit k sits at a bus of index from (k // 128) * 1024 to (k // 128 + 1) * 1024 - 1.
All inputs are finite; a program needn't handle non-finite values.
Results may differ from the reference program's by a relative error of at most 0.0003.
Values sent between devices are 32-bit elements; how exact they have to be, the bound alone decides.
No kernel may reach another device: no remote copies, remote signals or barrier semaphores. Data moves between devices by JAX's collectives and lax.ppermute only.
A program may use at most 64 MiB of HBM per device.

```python
import math
import jax
import jax.numpy as jnp
from jax import lax

LINES = 16384
BUSES = 8192
STORE_DEV = 128
PERIOD_LENGTH = 2048
STORES = 1024
BUS_DEV = 1024


def draw_retention(key, part):
    sampler_seeds = jax.random.split(jax.random.fold_in(key, 11), 6)
    slow = jax.random.uniform(sampler_seeds[0], (STORES,)) < 0.5
    kept_total = jax.random.uniform(sampler_seeds[1], (STORES,), minval=0.4, maxval=0.8)
    fast_rate = jax.random.uniform(sampler_seeds[2], (STORES,), minval=1.0 / 50.0, maxval=1.0 / 30.0)
    leakage_fraction = jnp.where(slow, -jnp.log(kept_total) / PERIOD_LENGTH, fast_rate)
    noisy_demand_series = jax.random.uniform(sampler_seeds[3], (PERIOD_LENGTH, STORES), minval=0.5, maxval=1.5)
    spike_withdrawal = jax.random.uniform(sampler_seeds[4], (PERIOD_LENGTH, 1)) < 3.0 / PERIOD_LENGTH
    congestion_penalty_value = jax.random.uniform(sampler_seeds[5], (PERIOD_LENGTH, STORES), minval=0.2, maxval=0.4)
    retained_charge = jnp.exp(-leakage_fraction[None, :] * noisy_demand_series) * jnp.where(spike_withdrawal, 1.0 - congestion_penalty_value, 1.0)
    return retained_charge.astype(jnp.float32)


def draw_storage_bus(key, part):
    position = jax.random.randint(jax.random.fold_in(key, 23), (STORES,), 0, BUS_DEV)
    position = position.at[0].set(0).at[STORES - 1].set(BUS_DEV - 1)
    owner = jnp.arange(STORES, dtype=jnp.int32) // STORE_DEV
    return (owner * BUS_DEV + position).astype(jnp.int32)


def touch_ends(entries, stream_key, least, high):
    longest = entries.shape.index(max(entries.shape))
    spots = []
    for shift in (0, 1):
        where = [jax.random.randint(jax.random.fold_in(stream_key, axis), (), 0, length) for axis, length in enumerate(entries.shape)]
        where[longest] = (where[longest] + shift) % entries.shape[longest]
        spots.append(tuple(where))
    return entries.at[spots[0]].set(least).at[spots[1]].set(high)


def steps_of(own_key, dims, cuts, smallest, high):
    loudness, own = 1.0, jax.random.fold_in(own_key, 6)
    for dim, parts in cuts:
        heights = jnp.exp(jax.random.uniform(jax.random.fold_in(own, dim), (parts,), jnp.float32, smallest / len(cuts), high / len(cuts)))
        loudness = loudness * jnp.repeat(heights, dims[dim] // parts).reshape([-1 if axis == dim else 1 for axis in range(len(dims))])
    return loudness


def gaussian(rng, extent, spread, limit, cuts=(), kind=jnp.bfloat16):
    drawn = jax.random.normal(rng, extent, jnp.float32) * spread
    if len(cuts) > 0:
        drawn = steps_of(rng, extent, cuts, -0.22, 0.18) * drawn
    return jnp.clip(drawn, min=-limit, max=limit).astype(kind)


def setup_inputs(seed: int = 0) -> dict:
    key_list = jax.random.split(jax.random.key(seed), 9)
    return {
        "injections": gaussian(key_list[0], (PERIOD_LENGTH, BUSES), 1.0, 6.0, ((0, 32), (1, 8)), jnp.float32),
        "shift_factors": gaussian(key_list[1], (LINES, BUSES), BUSES ** -0.5, 0.0625, ((0, 32), (1, 8)), jnp.float32),
        "line_rating": touch_ends(jax.random.randint(key_list[2], (PERIOD_LENGTH, LINES), 40, 160), jax.random.fold_in(key_list[2], 1), 40, 159).astype(jnp.int32),
        "retention": draw_retention(jax.random.fold_in(key_list[8], 71), 0),
        "discharge": jnp.clip(jnp.exp(math.log(0.5) - 2.3025851 * jax.random.uniform(key_list[4], (STORES,), jnp.float32) ** steps_of(key_list[4], (STORES,), ((0, 8),), -0.2, 0.2)), 0.05, 0.5),
        "profile": gaussian(key_list[5], (PERIOD_LENGTH, STORES), 1.0, 6.0, ((0, 32), (1, 8)), jnp.float32),
        "storage_bus": draw_storage_bus(jax.random.fold_in(key_list[8], 71), 0),
        "online_hour": touch_ends(jax.random.randint(key_list[7], (STORES,), 0, PERIOD_LENGTH // 2), jax.random.fold_in(key_list[7], 1), 0, (PERIOD_LENGTH // 2) - 1).astype(jnp.int32),
    }


def reference(injections, shift_factors, line_rating, retention, discharge, profile, storage_bus, online_hour):
    highest = lax.Precision.HIGHEST
    line_flows = jnp.dot(injections, shift_factors.T, precision=highest, preferred_element_type=jnp.float32)
    limits = line_rating.astype(jnp.float32) * 0.01
    excess = jnp.maximum(jnp.abs(line_flows) - limits, 0.0)
    flow_adjoint = excess * jnp.sign(line_flows)
    bus_adjoint = jnp.dot(flow_adjoint, shift_factors, precision=highest, preferred_element_type=jnp.float32)
    source = discharge[None, :] * bus_adjoint[:, storage_bus]

    def backward_step(carried, hour_inputs):
        source_now, keep_now = hour_inputs
        costate_now = source_now + carried
        return (keep_now * costate_now, costate_now)
    _, costate = lax.scan(backward_step, jnp.zeros((STORES,), jnp.float32), (source, retention), reverse=True)
    hour_index = jnp.arange(PERIOD_LENGTH, dtype=jnp.int32)
    active = (hour_index[:, None] >= online_hour[None, :]).astype(jnp.float32)
    size_grad = lax.optimization_barrier(jnp.sum(costate * profile * active, axis=0)) / math.sqrt(PERIOD_LENGTH)
    return (bus_adjoint, size_grad)
```

```python
import math

import jax
import jax.numpy as jnp
from jax import lax
from jax.sharding import Mesh, PartitionSpec as P


AXES = {"z": 8, "xh": 2, "core": 2, "xl": 2, "y": 4}
LINE = ("z", "xh", "core")
BUS = ("xl", "y")


def send(value, axes, target):
    sizes = [AXES[axis] for axis in axes]
    pairs = []
    for source in range(math.prod(sizes)):
        place, rest = ([], source)
        for size in reversed(sizes):
            place.insert(0, rest % size)
            rest //= size
        to = target(*place)
        goal = 0
        for size, part in zip(sizes, to, strict=True):
            goal = goal * size + part % size
        pairs.append((source, goal))
    return lax.ppermute(value, axes, pairs)


def flip(value, *axes):
    return send(value, axes, lambda *place: tuple(1 - p for p in place))


def shift(value, by):
    return send(value, ("z",), lambda z: (z + by,))


def pair_even(value):
    return send(value, ("y",), lambda y: (y ^ 1,))


def pair_odd(value):
    return send(value, ("y",), lambda y: (3 - y,))


def halves(value, bit):
    rows = value.shape[0] // 2
    keep = lax.dynamic_slice_in_dim(value, bit * rows, rows)
    give = lax.dynamic_slice_in_dim(value, (1 - bit) * rows, rows)
    return keep, give


def joined(mine, other, bit):
    return jnp.where(bit == 0, jnp.concatenate([mine, other]), jnp.concatenate([other, mine]))


def overload(line_flows, limits):
    excess = jnp.maximum(jnp.abs(line_flows) - limits, 0.0)
    return excess * jnp.sign(line_flows)


def combine(earlier, latter):
    return (latter[0] * earlier[0], latter[1] + latter[0] * earlier[1])


def total_adjoint(flows, ratings):
    y = lax.axis_index("y")
    outer = ((y == 1) | (y == 2)).astype(jnp.int32)
    upper = (y >= 2).astype(jnp.int32)
    odd = y % 2
    plans = ((pair_even, outer, pair_odd, upper), (pair_odd, upper, pair_even, odd))
    rows = flows.shape[0]
    parts = [flows[: rows // 2], flows[rows // 2 :]]
    rates = [ratings[: rows // 2], ratings[rows // 2 :]]
    for i, (first, bit, _, _) in enumerate(plans):
        keep, give = halves(parts[i], bit)
        parts[i] = keep + first(give)
        rates[i] = halves(rates[i], bit)[0]
    for i, (_, _, second, bit) in enumerate(plans):
        keep, give = halves(parts[i], bit)
        limits = halves(rates[i], bit)[0].astype(jnp.float32) * 0.01
        parts[i] = overload(keep + second(give), limits)
    for i, (_, _, second, bit) in enumerate(plans):
        parts[i] = joined(parts[i], second(parts[i]), bit)
    for i, (first, bit, _, _) in enumerate(plans):
        parts[i] = joined(parts[i], first(parts[i]), bit)
    return jnp.concatenate(parts)


def stored(retention, profile, online_hour):
    hour_dev = retention.shape[0]
    z, h, c = (lax.axis_index(axis) for axis in LINE)
    line = z * 4 + h * 2 + c
    hour = line * hour_dev + jnp.arange(hour_dev, dtype=jnp.int32)
    active = (hour[:, None] >= online_hour[None, :]).astype(jnp.float32)
    gain, offset = lax.associative_scan(combine, (retention, profile * active), axis=0)
    total = jnp.stack([gain[-1], offset[-1]])
    before = jnp.stack([jnp.ones_like(gain[-1]), jnp.zeros_like(gain[-1])])
    steps = (
        (c, lambda v: flip(v, "core")),
        (h, lambda v: flip(v, "xh")),
        (z % 2, lambda v: send(v, ("z",), lambda p: (p ^ 1,))),
        (z // 2 % 2, lambda v: send(v, ("z",), lambda p: (p ^ 2,))),
        (z // 4, lambda v: send(v, ("z",), lambda p: (p ^ 4,))),
    )
    for bit, exchange in steps:
        other = exchange(total)
        late = bit == 1
        before = jnp.where(late, jnp.stack(combine(other, before)), before)
        total = jnp.where(late, jnp.stack(combine(other, total)), jnp.stack(combine(total, other)))
    return offset + gain * before[1][None, :]


def sum_over_line(value):
    value = value + flip(value, "core")
    value = value + flip(value, "xh")
    for bit in (1, 2, 4):
        value = value + send(value, ("z",), lambda p, bit=bit: (p ^ bit,))
    return value


GROUPS = ((4,), (3, 5), (2, 6), (1, 7, 0))


def on_device(
    injections, shift_factors, line_rating, retention, discharge, profile, storage_bus, online_hour
):
    high, highest = (lax.Precision.HIGH, lax.Precision.HIGHEST)
    f32 = jnp.float32
    hour_dev, bus_dev = injections.shape
    half = hour_dev // 2
    z, h, c = (lax.axis_index(axis) for axis in LINE)
    l, y = (lax.axis_index(axis) for axis in BUS)

    def dot(a, b):
        return jnp.dot(a, b, precision=high, preferred_element_type=f32)

    def dot_t(a, b):
        return lax.dot_general(
            a, b, (((1,), (1,)), ((), ())), precision=high, preferred_element_type=f32
        )

    keep, give = halves(injections, l)
    near = flip(keep, "xh")
    across = flip(give, "xl")
    far = flip(give, "xh", "xl")
    mine = jnp.concatenate(
        [jnp.concatenate([keep, near]), jnp.concatenate([across, far])], axis=1
    )
    factors, _ = lax.optimization_barrier((shift_factors, (near, across, far)))
    other_factors = flip(factors, "xl")
    pieces = {0: mine}
    up, down = (mine, mine)
    for step in (1, 2, 3):
        up = shift(up, 1)
        down = shift(down, -1)
        pieces[8 - step], pieces[step] = (up, down)
    own4 = shift(up[:, :bus_dev], 1)
    oth4 = shift(down[:, bus_dev:], -1)
    split = {d: (p[:, :bus_dev], p[:, bus_dev:]) for d, p in pieces.items()}
    split[4] = (own4, oth4)
    both = {}
    for d in (0, 1, 7, 2, 6, 3, 5, 4):
        if d == 4:
            swapped = (flip(own4, "core"), flip(oth4, "core"))
        else:
            whole = flip(pieces[d], "core")
            swapped = (whole[:, :bus_dev], whole[:, bus_dev:])
        both[d] = tuple(jnp.concatenate(pair) for pair in zip(split[d], swapped, strict=True))

    weight = stored(retention, profile, online_hour)

    def ratings_of(d):
        blocks = []
        for f in (0, 1):
            for e in (0, 1):
                owner = ((z + d) % 8) * 4 + (h ^ e) * 2 + (c ^ f)
                blocks.append(
                    lax.dynamic_slice_in_dim(line_rating, owner * hour_dev + l * half, half)
                )
        return jnp.concatenate(blocks)

    sums = {}
    for group in GROUPS:
        own = jnp.concatenate([both[d][0] for d in group])
        oth = jnp.concatenate([both[d][1] for d in group])
        flows = dot_t(own, shift_factors) + dot_t(oth, other_factors)
        ratings = jnp.concatenate([ratings_of(d) for d in group])
        adjoint = total_adjoint(flows, ratings)
        g_own = dot(adjoint, shift_factors)
        g_oth = dot(adjoint, other_factors)
        for i, d in enumerate(group):
            at = i * 4 * half
            first = slice(at, at + 2 * half)
            second = slice(at + 2 * half, at + 4 * half)
            gathered = jnp.concatenate([g_own[second], g_oth[second]], axis=1)
            sums[d] = jnp.concatenate([g_own[first], g_oth[first]], axis=1) + flip(gathered, "core")

    up = shift(sums[4][:, :bus_dev], 1)
    down = shift(sums[4][:, bus_dev:], -1)
    up = shift(jnp.concatenate([sums[3][:, :bus_dev] + up, sums[3][:, bus_dev:]], axis=1), 1)
    down = shift(jnp.concatenate([sums[5][:, :bus_dev], sums[5][:, bus_dev:] + down], axis=1), -1)
    up = shift(sums[2] + up, 1)
    down = shift(sums[6] + down, -1)
    up = shift(sums[1] + up, 1)
    down = shift(sums[7] + down, -1)
    last = sums[0] + up + down
    near = flip(last[half:, :bus_dev], "xh")
    across = flip(last[:half, bus_dev:], "xl")
    far = flip(last[half:, bus_dev:], "xh", "xl")
    bus_adjoint = joined(last[:half, :bus_dev] + near, across + far, l)

    local_bus = storage_bus - (l * 4 + y) * bus_dev
    onehot = (jnp.arange(bus_dev, dtype=jnp.int32)[:, None] == local_bus[None, :]).astype(f32)
    at_stores = jnp.dot(bus_adjoint, onehot, precision=highest, preferred_element_type=f32)
    partial = jnp.sum(weight * at_stores, axis=0)
    hours = hour_dev * 32
    size_grad = sum_over_line(discharge * partial) / math.sqrt(hours)
    return (bus_adjoint, size_grad)


def solution(mesh):
    fine = Mesh(mesh.devices.reshape(tuple(AXES.values())), tuple(AXES))
    in_specs = (
        P(LINE, BUS),
        P(LINE, BUS),
        P(None, LINE),
        P(LINE, BUS),
        P(BUS),
        P(LINE, BUS),
        P(BUS),
        P(BUS),
    )
    out_specs = (P(LINE, BUS), P(BUS))
    return jax.shard_map(
        on_device, mesh=fine, in_specs=in_specs, out_specs=out_specs, check_vma=False
    )
```
